32 devices in a mesh: chi: 4 (over y, x), dl: 4 (over z), cell: 2 (over core).
Axes of the slice: x: 2, y: 2, z: 4, core: 2. Of those that a mesh axis runs over, the one named last changes fastest.
Arguments:
- left_env: bfloat16 [2, 512, 512, 36], P('cell', None, 'chi'), may hold values from -6 to 6
- up_left: bfloat16 [2, 512, 36, 512], P('cell', 'chi', None, 'dl'), may hold values from -0.109375 to 0.109375
- up_center: bfloat16 [2, 512, 36, 512], P('cell', 'chi', None, 'dl'), may hold values from -0.109375 to 0.109375
- right_env: bfloat16 [2, 512, 36, 512], P('cell', 'dl'), may hold values from -0.046875 to 0.046875
- center: bfloat16 [2, 512, 512], P('cell', None, 'dl'), may hold values from -0.25 to 0.25
- ket_tensor: bfloat16 [2, 6, 6, 6, 6, 2], P('cell'), may hold values from -0.875 to 0.875
Outputs:
- left_env_new: float32 [2, 512, 36, 512], P('cell', 'chi', None, 'dl')
- new_left: float32 [2, 512, 36, 512], P('cell', 'chi', None, 'dl')
The draws below stay inside these ranges and needn't reach their ends.
All inputs are finite; a program needn't handle non-finite values.
Results may differ from the reference program's by a relative error of at most 0.0066.
The reference program's roundings to bfloat16 on the way count: a program that leaves them out, or rounds other values in their place, can miss the bound.
Values may be sent and summed in bfloat16 or wider, within the bound.
A program may use at most 256 MiB of HBM per device.

```python
import math
import jax
import jax.numpy as jnp
from jax import lax

CHI = 512
D = 6
PHYS = 2
ITERS = 5
DL = 36
ROWS = 2


def block_scale(rng, shape, cuts, low, high):
    def one(position, blocks):
        draws = jax.random.uniform(jax.random.fold_in(jax.random.fold_in(rng, 6), position), (blocks,), jnp.float32, low / len(cuts), high / len(cuts))
        return jnp.repeat(jnp.exp(draws), shape[position] // blocks).reshape((-1,) + (1,) * (len(shape) - position - 1))

    factor_of = one(*cuts[0])
    for cut in cuts[1:]:
        factor_of = factor_of * one(*cut)
    return factor_of


def normal_values(stream_key, dims, deviation, reach, split=(), kind=jnp.bfloat16):
    entries = jax.random.normal(stream_key, dims, jnp.float32) * deviation
    if len(split) > 0:
        entries = block_scale(stream_key, dims, split, -0.22, 0.18) * entries
    return jnp.clip(entries, min=-reach, max=reach).astype(kind)


def setup_inputs(seed: int = 0) -> dict:
    key_list = jax.random.split(jax.random.key(seed), 7)
    left_env = normal_values(key_list[0], (ROWS, CHI, CHI, DL), 1.0, 6.0, ((0, 2), (2, 4)))
    up_left = normal_values(key_list[1], (ROWS, CHI, DL, CHI), (CHI * D) ** -0.5, 0.109375, ((0, 2), (1, 4), (3, 4)))
    up_center = normal_values(key_list[2], (ROWS, CHI, DL, CHI), (CHI * D) ** -0.5, 0.109375, ((0, 2), (1, 4), (3, 4)))
    right_env = normal_values(key_list[3], (ROWS, CHI, DL, CHI), (CHI * DL) ** -0.5, 0.046875, ((0, 2), (1, 4)))
    center = normal_values(key_list[4], (ROWS, CHI, CHI), CHI ** -0.5, 0.25, ((0, 2), (2, 4)))
    ket_tensor = normal_values(key_list[5], (ROWS, D, D, D, D, PHYS), 50 ** -0.5, 0.875, ((0, 2),))
    return {"left_env": left_env, "up_left": up_left, "up_center": up_center, "right_env": right_env, "center": center, "ket_tensor": ket_tensor}


HIGHEST = lax.Precision.HIGHEST

def layered(block, tensor):
    leg_size = tensor.shape[0]
    amount = block.shape[0]
    columns = block.shape[3]
    unfolded = block.reshape(amount, leg_size, leg_size, leg_size, leg_size, columns).astype(jnp.float32)
    tensor_f = tensor.astype(jnp.float32)
    ket_side = jnp.einsum('blLuUc,lurdp->bLUcrdp', unfolded, tensor_f).astype(jnp.bfloat16)
    both_sides = jnp.einsum('bLUcrdp,LUsep->brsdec', ket_side.astype(jnp.float32), tensor_f)
    return both_sides.reshape(amount, leg_size * leg_size, leg_size * leg_size, columns).astype(jnp.bfloat16)

def one_row(env_left, left_iso, left_mid, env_right, bond_mat, site_ket, bra_iso):
    chi_all = env_left.shape[0]
    leg_width = env_left.shape[2]
    stride = min(chi_all, 32)
    blocks = chi_all // stride
    env_blocks = jnp.moveaxis(env_left.reshape(chi_all, blocks, stride, leg_width), 1, 0)
    bra_blocks = bra_iso.reshape(blocks, stride, leg_width, chi_all)
    iso_f = left_iso.astype(jnp.float32)
    mid_f = left_mid.astype(jnp.float32)
    right_f = env_right.astype(jnp.float32)

    def visit(running, pieces):
        env_block, bra_block = pieces
        env_f = env_block.astype(jnp.float32)
        left_x = jnp.einsum('abm,asc->bmsc', env_f, iso_f).astype(jnp.bfloat16)
        right_x = jnp.einsum('abm,asc->bmsc', env_f, mid_f).astype(jnp.bfloat16)
        left_cut = layered(left_x, site_ket)
        right_cut = layered(right_x, site_ket)
        running = running + jnp.einsum('bmdc,bdk->kmc', left_cut.astype(jnp.float32), bra_block.astype(jnp.float32))
        center_piece = jnp.einsum('bmda,amc->cbd', right_cut.astype(jnp.float32), right_f)
        return (running, center_piece)
    initial = jnp.zeros((chi_all, leg_width, chi_all), jnp.float32)
    env_new, center_pieces = lax.scan(visit, initial, (env_blocks, bra_blocks))
    center_new = jnp.moveaxis(center_pieces, 0, 1).reshape(chi_all, chi_all, leg_width).astype(jnp.bfloat16)
    mixed = jnp.einsum('abm,ax->bmx', env_left.astype(jnp.float32), bond_mat.astype(jnp.float32)).astype(jnp.bfloat16)
    bond_new = jnp.einsum('bma,amc->cb', mixed.astype(jnp.float32), right_f).astype(jnp.bfloat16)
    target = jnp.einsum('cbd,cx->bdx', center_new.astype(jnp.float32), bond_new.astype(jnp.float32))
    flat_target = target.reshape(chi_all * leg_width, chi_all)
    current = flat_target * (0.25 * math.sqrt(chi_all) / jnp.sqrt(jnp.sum(flat_target * flat_target)))
    for sweep_index in range(ITERS):
        gram_mat = jnp.dot(current.T, current, precision=HIGHEST)
        current = 1.5 * current - 0.5 * jnp.dot(current, gram_mat, precision=HIGHEST)
    new_left = (current * math.sqrt(chi_all * leg_width)).reshape(chi_all, leg_width, chi_all)
    return (env_new, new_left)

def reference(left_env, up_left, up_center, right_env, center, ket_tensor):
    env_list = []
    left_list = []
    for row_index in range(ROWS):
        next_index = (row_index + 1) % ROWS
        env_new, new_left = one_row(left_env[row_index], up_left[row_index], up_center[row_index], right_env[row_index], center[row_index], ket_tensor[row_index], up_left[next_index])
        env_list.append(env_new)
        left_list.append(new_left)
    return (jnp.stack(env_list), jnp.stack(left_list))
```

```python
import math

import jax
import jax.numpy as jnp
from jax import lax
from jax.sharding import PartitionSpec as P

ITERS = 5


HIGH = lax.Precision.HIGH
F32 = jnp.float32
BF16 = jnp.bfloat16


def from_behind(block, axis, distance):
    devices = range(lax.axis_size(axis))
    route = [((i - distance) % len(devices), i) for i in devices]
    return lax.ppermute(block, axis, route)


def pick(rows, cols, row_of, col_of):
    r = lax.broadcasted_iota(jnp.int32, (rows, cols), 0)
    c = lax.broadcasted_iota(jnp.int32, (rows, cols), 1)
    return (row_of(r) == col_of(c)).astype(BF16)


def double_layer(tensor, pad):
    leg = tensor.shape[0]
    two = leg * leg
    phys = tensor.shape[4]
    big = two * pad

    def outer(first):
        def code(n):
            m, s = n // pad, n % pad
            a = m // leg if first else m % leg
            b = s // leg if first else s % leg
            return jnp.where(s < two, a * leg + b, -1)

        return code

    def same(n):
        return n

    total = None
    ket_rows = pick(big, two, outer(True), same)
    bra_rows = pick(big, two, outer(False), same)
    for p in range(phys):
        mat = tensor[:, :, :, :, p].reshape(two, two)
        ket_small = jnp.dot(ket_rows, mat, preferred_element_type=F32).astype(BF16)
        bra_small = jnp.dot(bra_rows, mat, preferred_element_type=F32).astype(BF16)
        ket = lax.dot_general(ket_small, ket_rows, (((1,), (1,)), ((), ())), preferred_element_type=F32)
        bra = lax.dot_general(bra_small, bra_rows, (((1,), (1,)), ((), ())), preferred_element_type=F32)
        total = ket * bra if total is None else total + ket * bra
    return total.astype(BF16)


def through_site(env, stacked, layer, pad):
    two = env.shape[2]
    summed = jnp.einsum("abm,asc->bmsc", env, stacked, preferred_element_type=F32).astype(BF16)
    amount, columns = summed.shape[0], summed.shape[3]
    flat = summed.reshape(amount, two * pad, columns)
    out = jnp.einsum("tn,btc->bnc", layer, flat, preferred_element_type=F32).astype(BF16)
    return out.reshape(amount, two, pad, columns)


def shards(left_env, up_left, up_center, right_env, center, ket_tensor):
    env_local = left_env[0]
    left_iso = up_left[0]
    left_mid = up_center[0]
    env_right = right_env[0]
    bond_mat = center[0]
    site_ket = ket_tensor[0]
    chi_all = env_local.shape[0]
    leg_width = env_local.shape[2]
    pad = -(-leg_width // 8) * 8
    widen = ((0, 0), (0, pad - leg_width), (0, 0))
    rows = left_iso.shape[0]
    col_count = left_iso.shape[2]

    mid_all = lax.all_gather(left_mid, "chi", axis=0, tiled=True)
    iso_all = lax.all_gather(left_iso, "chi", axis=0, tiled=True)
    next_iso = from_behind(left_iso, "cell", -1)
    bra_iso = lax.all_gather(next_iso, "dl", axis=2, tiled=True)

    layer = double_layer(site_ket, pad)

    mixed = jnp.einsum("abm,ax->bmx", env_local, bond_mat, preferred_element_type=F32).astype(BF16)
    bond_term = jnp.einsum("bma,amc->bc", mixed, env_right, preferred_element_type=F32)
    bond_slots = lax.dynamic_update_slice(
        jnp.zeros((chi_all, chi_all), F32), bond_term, (lax.axis_index("chi") * rows, 0)
    )
    bond_full = lax.psum(bond_slots, ("chi", "dl")).astype(BF16)

    right_cut = through_site(env_local, jnp.pad(mid_all, widen), layer, pad)
    center_term = jnp.einsum(
        "bmda,amc->bdc", right_cut[:, :, :leg_width], env_right, preferred_element_type=F32
    ).astype(BF16)
    iso_all, center_term = lax.optimization_barrier((iso_all, center_term))
    center_part = lax.psum_scatter(center_term, "dl", scatter_dimension=0, tiled=True)
    cross = lax.psum(
        jnp.einsum("bdc,bdy->cy", center_part, center_part, preferred_element_type=F32),
        ("chi", "dl"),
    )
    center_all = lax.all_gather(center_part, "dl", axis=0, tiled=True)

    left_cut = through_site(env_local, jnp.pad(iso_all, widen), layer, pad)
    env_term = jnp.einsum(
        "bmdc,bdk->kmc", left_cut[:, :, :leg_width], bra_iso, preferred_element_type=F32
    ).astype(BF16)
    env_new = lax.psum_scatter(env_term, "chi", scatter_dimension=0, tiled=True).astype(F32)

    bond_wide = bond_full.astype(F32)
    gram = jnp.dot(
        jnp.dot(bond_wide, cross, precision=HIGH), bond_wide.T, precision=HIGH
    )
    one = jnp.eye(chi_all, dtype=F32)
    norm_sum = jnp.sum(gram * one)
    factor = 0.25 * math.sqrt(chi_all) / jnp.sqrt(norm_sum)
    gram = gram * (factor * factor)
    product = None
    for sweep_index in range(ITERS):
        step = 1.5 * one - 0.5 * gram
        product = step if product is None else jnp.dot(product, step, precision=HIGH)
        if sweep_index < ITERS - 1:
            gram = jnp.dot(jnp.dot(step, gram, precision=HIGH), step, precision=HIGH)
    mine = lax.dynamic_slice_in_dim(product, lax.axis_index("dl") * col_count, col_count, 1)
    weight = lax.dot_general(bond_wide, mine, (((0,), (0,)), ((), ())), precision=HIGH)
    weight = weight * (factor * math.sqrt(chi_all * leg_width))
    new_left = jnp.einsum("bdc,cx->bdx", center_all.astype(F32), weight, precision=HIGH)
    return (env_new[None], new_left[None])


def solution(mesh):
    placed = (
        P("cell", None, "chi", None),
        P("cell", "chi", None, "dl"),
        P("cell", "chi", None, "dl"),
        P("cell", "dl", None, None),
        P("cell", None, "dl"),
        P("cell", None, None, None, None, None),
    )
    return jax.shard_map(
        shards,
        mesh=mesh,
        in_specs=placed,
        out_specs=(P("cell", "chi", None, "dl"), P("cell", "chi", None, "dl")),
        check_vma=False,
    )
```

```python
import math

import jax
import jax.numpy as jnp
from jax import lax
from jax.experimental.layout import Layout, with_layout_constraint
from jax.sharding import PartitionSpec as P

ITERS = 5


HIGH = lax.Precision.HIGH
F32 = jnp.float32
BF16 = jnp.bfloat16


def from_behind(block, axis, distance):
    devices = range(lax.axis_size(axis))
    route = [((i - distance) % len(devices), i) for i in devices]
    return lax.ppermute(block, axis, route)


def pick(rows, cols, row_of, col_of):
    r = lax.broadcasted_iota(jnp.int32, (rows, cols), 0)
    c = lax.broadcasted_iota(jnp.int32, (rows, cols), 1)
    return (row_of(r) == col_of(c)).astype(BF16)


def double_layer(tensor, pad):
    leg = tensor.shape[0]
    two = leg * leg
    phys = tensor.shape[4]
    big = two * pad

    def outer(first):
        def code(n):
            m, s = n // pad, n % pad
            a = m // leg if first else m % leg
            b = s // leg if first else s % leg
            return jnp.where(s < two, a * leg + b, -1)

        return code

    def same(n):
        return n

    total = None
    ket_rows = pick(big, two, outer(True), same)
    bra_rows = pick(big, two, outer(False), same)
    for p in range(phys):
        mat = tensor[:, :, :, :, p].reshape(two, two)
        ket_small = jnp.dot(ket_rows, mat, preferred_element_type=F32).astype(BF16)
        bra_small = jnp.dot(bra_rows, mat, preferred_element_type=F32).astype(BF16)
        ket = lax.dot_general(ket_small, ket_rows, (((1,), (1,)), ((), ())), preferred_element_type=F32)
        bra = lax.dot_general(bra_small, bra_rows, (((1,), (1,)), ((), ())), preferred_element_type=F32)
        total = ket * bra if total is None else total + ket * bra
    return total.astype(BF16)


def row_major(block):
    return with_layout_constraint(block, Layout(major_to_minor=tuple(range(block.ndim))))


def site_input(env, stacked):
    summed = jnp.einsum("abm,csa->cmsb", env, stacked, preferred_element_type=F32).astype(BF16)
    summed = row_major(summed)
    columns, two, pad, amount = summed.shape
    return summed.reshape(columns, two * pad, amount)


def site_output(flat, layer, pad):
    out = jnp.einsum("tn,ctb->cnb", layer, flat, preferred_element_type=F32).astype(BF16)
    return out.reshape(out.shape[0], out.shape[1] // pad, pad, out.shape[2])


def spread_rows(block, pad):
    turned = jnp.pad(block.transpose(2, 1, 0), ((0, 0), (0, pad - block.shape[1]), (0, 0)))
    return lax.all_gather(row_major(turned), "chi", axis=2, tiled=True)


def shards(left_env, up_left, up_center, right_env, center, ket_tensor):
    env_local = left_env[0]
    left_iso = up_left[0]
    left_mid = up_center[0]
    env_right = right_env[0]
    bond_mat = center[0]
    site_ket = ket_tensor[0]
    chi_all = env_local.shape[0]
    leg_width = env_local.shape[2]
    pad = -(-leg_width // 8) * 8
    rows = left_iso.shape[0]
    col_count = left_iso.shape[2]

    mid_all = spread_rows(left_mid, pad)
    iso_all = spread_rows(left_iso, pad)
    next_iso = from_behind(left_iso, "cell", -1)
    bra_iso = lax.all_gather(next_iso, "dl", axis=2, tiled=True)

    layer = double_layer(site_ket, pad)

    mixed = jnp.einsum("abm,ax->bmx", env_local, bond_mat, preferred_element_type=F32).astype(BF16)
    bond_term = jnp.einsum("bma,amc->bc", mixed, env_right, preferred_element_type=F32)
    bond_slots = lax.dynamic_update_slice(
        jnp.zeros((chi_all, chi_all), F32), bond_term, (lax.axis_index("chi") * rows, 0)
    )
    mid_all, bond_slots = lax.optimization_barrier((mid_all, bond_slots))
    bond_sum = lax.psum(bond_slots, ("chi", "dl"))

    right_cut = site_output(site_input(env_local, mid_all), layer, pad)
    center_term = jnp.einsum(
        "amdb,amc->bdc", right_cut[:, :, :leg_width], env_right, preferred_element_type=F32
    ).astype(BF16)
    iso_all, center_term, bond_sum = lax.optimization_barrier((iso_all, center_term, bond_sum))
    bond_full = bond_sum.astype(BF16)
    center_part = lax.psum_scatter(center_term, "dl", scatter_dimension=0, tiled=True)
    cross_part = jnp.einsum("bdc,bdy->cy", center_part, center_part, preferred_element_type=F32)

    def env_piece(cut):
        term = jnp.einsum(
            "cmdb,bdk->kmc", cut[:, :, :leg_width], bra_iso, preferred_element_type=F32
        ).astype(BF16)
        return lax.psum_scatter(term, "chi", scatter_dimension=0, tiled=True).astype(F32)

    half = (leg_width // 2) * pad
    left_flat = site_input(env_local, iso_all)
    left_early = site_output(left_flat, layer[:, :half], pad)
    left_early, left_flat, cross_part, center_part = lax.optimization_barrier(
        (left_early, left_flat, cross_part, center_part)
    )
    cross = lax.psum(cross_part, ("chi", "dl"))
    center_all = lax.all_gather(center_part, "dl", axis=0, tiled=True)
    left_late = site_output(left_flat, layer[:, half:], pad)
    env_new = jnp.concatenate([env_piece(left_early), env_piece(left_late)], axis=1)

    bond_wide = bond_full.astype(F32)
    gram = jnp.dot(
        jnp.dot(bond_wide, cross, precision=HIGH), bond_wide.T, precision=HIGH
    )
    one = jnp.eye(chi_all, dtype=F32)
    norm_sum = jnp.sum(gram * one)
    factor = 0.25 * math.sqrt(chi_all) / jnp.sqrt(norm_sum)
    gram = gram * (factor * factor)
    product = None
    for sweep_index in range(ITERS):
        step = 1.5 * one - 0.5 * gram
        product = step if product is None else jnp.dot(product, step, precision=HIGH)
        if sweep_index < ITERS - 1:
            gram = jnp.dot(jnp.dot(step, gram, precision=HIGH), step, precision=HIGH)
    mine = lax.dynamic_slice_in_dim(product, lax.axis_index("dl") * col_count, col_count, 1)
    weight = lax.dot_general(bond_wide, mine, (((0,), (0,)), ((), ())), precision=HIGH)
    weight = weight * (factor * math.sqrt(chi_all * leg_width))
    new_left = jnp.einsum("bdc,cx->bdx", center_all.astype(F32), weight, precision=HIGH)
    return (env_new[None], new_left[None])


def solution(mesh):
    placed = (
        P("cell", None, "chi", None),
        P("cell", "chi", None, "dl"),
        P("cell", "chi", None, "dl"),
        P("cell", "dl", None, None),
        P("cell", None, "dl"),
        P("cell", None, None, None, None, None),
    )
    return jax.shard_map(
        shards,
        mesh=mesh,
        in_specs=placed,
        out_specs=(P("cell", "chi", None, "dl"), P("cell", "chi", None, "dl")),
        check_vma=False,
    )
```
